32 devices in a mesh: row: 8 (over y, x, core), col: 4 (over z).
Axes of the slice: x: 2, y: 2, z: 4, core: 2. Of those that a mesh axis runs over, the one named last changes fastest.
Arguments:
- transitions: bfloat16 [4, 1024, 32768], P(None, 'row', 'col'), may hold values from 1.5199184e-06 to 0.00015258789
- values: bfloat16 [32768, 6144], P('row', 'col'), may hold values from -1280 to 1280
- earlier_sum: bfloat16 [4, 1024, 6144], P(None, 'row', 'col'), may hold values from -8 to 8
- section_costs: bfloat16 [4, 1024, 6144], P(None, 'row', 'col'), may hold values from 0 to 3
Outputs:
- backed_up: float32 [1024, 6144], P('row', 'col')
The draws below stay inside these ranges and needn't reach their ends.
All inputs are finite; a program needn't handle non-finite values.
Results may differ from the reference program's by a relative error of at most 0.0003.
Values may be sent and summed in bfloat16 or wider, within the bound.
A program may use at most 192 MiB of HBM per device.

```python
import math
import jax
import jax.numpy as jnp
from jax import lax

S = 32768
A = 4
STEPS = 4
ROWS_DEV = 128
ROWS = 1024
M = 6144
N_ROW = 8


def levels(key, shape, cuts, least, largest):
    loudness = 1.0
    for axis_at, parts in cuts:
        steps = jax.random.uniform(jax.random.fold_in(jax.random.fold_in(key, 6), axis_at), (parts,), jnp.float32, least / len(cuts), largest / len(cuts))
        loudness = loudness * jnp.repeat(jnp.exp(steps), shape[axis_at] // parts).reshape((-1,) + (1,) * (len(shape) - 1 - axis_at))
    return loudness


def normal_values(own_key, extent, spread, reach, shards=(), held_as=jnp.bfloat16):
    entries = spread * jax.random.normal(own_key, extent, jnp.float32)
    if shards:
        entries = entries * levels(own_key, extent, shards, -0.22, 0.18)
    return jnp.clip(entries, -reach, reach).astype(held_as)


def setup_inputs(seed: int = 0) -> dict:
    arg_keys = jax.random.split(jax.random.key(seed), 5)
    return {
        "transitions": jnp.clip(jnp.exp(math.log(0.00015258789) - 4.609084 * jax.random.uniform(arg_keys[0], (A, ROWS, S), jnp.float32) ** levels(arg_keys[0], (A, ROWS, S), ((1, 8), (2, 4)), -0.2, 0.2)), 1.519918441772461e-06, 0.00015258789).astype(jnp.bfloat16),
        "values": normal_values(arg_keys[1], (S, M), (0.6 * S / (STEPS * S // 16) ** 0.5), 1280.0, ((0, 8), (1, 4))),
        "earlier_sum": normal_values(arg_keys[2], (A, ROWS, M), 1.5, 8.0, ((1, 8), (2, 4))),
        "section_costs": jnp.clip(3.0 * jax.random.uniform(arg_keys[3], (A, ROWS, M), jnp.float32) ** levels(arg_keys[3], (A, ROWS, M), ((1, 8), (2, 4)), -0.2, 0.2), 0.0, 3.0).astype(jnp.bfloat16),
    }


DISCOUNT = 0.97


def window_rows(transitions, values, index):
    block_width = S // N_ROW
    rows = lax.dynamic_slice_in_dim(transitions, index * ROWS_DEV, ROWS_DEV, 1)
    total = jnp.zeros((A, ROWS_DEV, values.shape[1]), jnp.float32)
    for section in range(STEPS):
        column_block = ((index + section) % N_ROW).astype(jnp.int32)
        chosen = lax.dynamic_slice_in_dim(rows, column_block * block_width, block_width, 2).astype(jnp.float32)
        states = lax.dynamic_slice_in_dim(values, column_block * block_width, block_width, 0).astype(jnp.float32)
        total = total + jnp.einsum("ars,sm->arm", chosen, states, precision=lax.Precision.HIGHEST)
    return total


def reference(transitions, values, earlier_sum, section_costs):
    indices = jnp.arange(N_ROW, dtype=jnp.int32)
    sums = lax.map(lambda index: window_rows(transitions, values, index), indices)
    window_sum = jnp.transpose(sums, (1, 0, 2, 3)).reshape(A, ROWS_DEV * N_ROW, values.shape[1])
    backup = earlier_sum.astype(jnp.float32) + window_sum
    return jnp.min(section_costs.astype(jnp.float32) + DISCOUNT * backup, axis=0)
```

```python
import functools

import jax
import jax.numpy as jnp
from jax import lax
from jax.experimental import pallas as pl
from jax.experimental.pallas import tpu as pltpu
from jax.sharding import PartitionSpec as P

STEPS = 4
PIECES = 2
DISCOUNT = 0.97
MESH = pl.DeviceIdType.MESH


def kernel(
    rows, cols, t_ref, v_ref, e_ref, c_ref, out_ref,
    slots, v_buf, work, arrived, e_buf, c_buf,
    in_sem, own_sem, slot_sem, first_sem, up_sem, down_sem, sum_send, sum_recv,
):
    b = lax.axis_index("row")
    z = lax.axis_index("col")
    ratio = rows // cols
    q = b // ratio
    actions = t_ref.shape[0]
    width = v_ref.shape[0]
    half = width // PIECES
    sums = (STEPS - 1) * actions
    total = STEPS * actions

    loads = [
        pltpu.make_async_copy(v_ref, v_buf, in_sem.at[0]),
        pltpu.make_async_copy(e_ref, e_buf, in_sem.at[1]),
        pltpu.make_async_copy(c_ref, c_buf, in_sem.at[2]),
    ]
    for load in loads:
        load.start()

    barrier = pltpu.get_barrier_semaphore()
    for d in range(1, STEPS):
        for by in (d, rows - d):
            pl.semaphore_signal(barrier, inc=1, device_id=((b + by) % rows, z), device_id_type=MESH)

    @pl.when(z > 0)
    def _():
        pl.semaphore_signal(barrier, inc=1, device_id=(b, z - 1), device_id_type=MESH)

    @pl.when(z < cols - 1)
    def _():
        pl.semaphore_signal(barrier, inc=1, device_id=(b, z + 1), device_id_type=MESH)

    beside = jnp.where(z > 0, 1, 0) + jnp.where(z < cols - 1, 1, 0)
    pl.semaphore_wait(barrier, 2 * (STEPS - 1) + beside)

    def held(j, a, h):
        offset = pl.multiple_of(j * width + h * half, 128)
        return t_ref.at[a, :, pl.ds(offset, half)]

    def first_copy(j, d, a, h):
        i = (d - 1) * actions + a
        return pltpu.make_async_remote_copy(
            src_ref=held(j, a, h), dst_ref=slots.at[i, h],
            send_sem=first_sem.at[j, a, h], recv_sem=slot_sem.at[i, h],
            device_id=(z * ratio + j, z), device_id_type=MESH,
        )

    def own_copy(j, a, h):
        i = (STEPS - 1) * actions + a
        return pltpu.make_async_copy(held(j, a, h), slots.at[i, h], own_sem.at[a, h])

    def for_blocks(away, own):
        for j in range(ratio):
            d = (z * ratio + j - b + rows) % rows

            @pl.when((d > 0) & (d < STEPS))
            def _():
                @pl.loop(0, actions)
                def _(a):
                    for h in range(PIECES):
                        away(j, d, a, h)

            if own is not None:
                @pl.when(d == 0)
                def _():
                    @pl.loop(0, actions)
                    def _(a):
                        for h in range(PIECES):
                            own(j, a, h)

    for_blocks(
        lambda j, d, a, h: first_copy(j, d, a, h).start(),
        lambda j, a, h: own_copy(j, a, h).start(),
    )

    def along(i, h, by, sem):
        return pltpu.make_async_remote_copy(
            src_ref=slots.at[i, h], dst_ref=slots.at[i, h],
            send_sem=sem.at[i, h], recv_sem=slot_sem.at[i, h],
            device_id=(b, z + by), device_id_type=MESH,
        )

    goes_up = (z >= q) & (z < cols - 1)
    goes_down = (z <= q) & (z > 0)

    def sum_copy(i):
        d = i // actions + 1
        return pltpu.make_async_remote_copy(
            src_ref=work.at[i], dst_ref=arrived.at[i],
            send_sem=sum_send.at[i], recv_sem=sum_recv.at[i],
            device_id=((b - d + rows) % rows, z), device_id_type=MESH,
        )

    loads[0].wait()

    @pl.loop(0, total)
    def _(i):
        for h in range(PIECES):
            local = (i >= sums) & (z == q)

            @pl.when(local)
            def _():
                own_copy(b % ratio, i % actions, h).wait()

            @pl.when(jnp.logical_not(local))
            def _():
                along(i, h, 0, up_sem).wait_recv()

            @pl.when(goes_up)
            def _():
                along(i, h, 1, up_sem).start()

            @pl.when(goes_down)
            def _():
                along(i, h, -1, down_sem).start()

            tile = 512

            @pl.loop(0, work.shape[2] // tile)
            def _(n):
                at = pl.ds(pl.multiple_of(n * tile, tile), tile)
                product = jnp.dot(
                    slots[i, h], v_buf[h * half:(h + 1) * half, at],
                    preferred_element_type=jnp.float32,
                )
                if h == 0:
                    work[i, :, at] = product
                else:
                    work[i, :, at] += product

        @pl.when((i >= 1) & (i <= sums))
        def _():
            sum_copy(i - 1).start()

    loads[1].wait()
    loads[2].wait()

    @pl.loop(0, sums)
    def _(i):
        sum_copy(i).wait_recv()

    @pl.loop(0, out_ref.shape[0] // 16)
    def _(k):
        at = pl.ds(pl.multiple_of(k * 16, 16), 16)
        best = None
        for a in range(actions):
            backup = e_buf[a, at, :].astype(jnp.float32) + work[sums + a, at, :]
            for d in range(STEPS - 1):
                backup = backup + arrived[d * actions + a, at, :]
            cost = c_buf[a, at, :].astype(jnp.float32) + DISCOUNT * backup
            best = cost if best is None else jnp.minimum(best, cost)
        out_ref[at, :] = best

    @pl.loop(0, sums)
    def _(i):
        sum_copy(i).wait_send()

    for_blocks(lambda j, d, a, h: first_copy(j, d, a, h).wait_send(), None)

    @pl.when(goes_up)
    def _():
        @pl.loop(0, total)
        def _(i):
            for h in range(PIECES):
                along(i, h, 1, up_sem).wait_send()

    @pl.when(goes_down)
    def _():
        @pl.loop(0, total)
        def _(i):
            for h in range(PIECES):
                along(i, h, -1, down_sem).wait_send()


def local(transitions, values, earlier_sum, section_costs):
    rows = lax.axis_size("row")
    cols = lax.axis_size("col")
    actions, height, _ = transitions.shape
    width, scenarios = values.shape
    total = STEPS * actions
    sums = (STEPS - 1) * actions
    ratio = rows // cols
    anywhere = pl.BlockSpec(memory_space=pl.ANY)
    dma = pltpu.SemaphoreType.DMA
    return pl.pallas_call(
        functools.partial(kernel, rows, cols),
        out_shape=jax.ShapeDtypeStruct((height, scenarios), jnp.float32),
        in_specs=[anywhere] * 4,
        out_specs=pl.BlockSpec(memory_space=pltpu.VMEM),
        scratch_shapes=[
            pltpu.VMEM((total, PIECES, height, width // PIECES), jnp.bfloat16),
            pltpu.VMEM((width, scenarios), jnp.bfloat16),
            pltpu.VMEM((total, height, scenarios), jnp.float32),
            pltpu.VMEM((sums, height, scenarios), jnp.float32),
            pltpu.VMEM((actions, height, scenarios), jnp.bfloat16),
            pltpu.VMEM((actions, height, scenarios), jnp.bfloat16),
            dma((3,)),
            dma((actions, PIECES)),
            dma((total, PIECES)),
            dma((ratio, actions, PIECES)),
            dma((total, PIECES)),
            dma((total, PIECES)),
            dma((sums,)),
            dma((sums,)),
        ],
        compiler_params=pltpu.CompilerParams(
            collective_id=0, has_side_effects=True, vmem_limit_bytes=66_000_000
        ),
    )(transitions, values, earlier_sum, section_costs)


def solution(mesh):
    in_specs = (
        P(None, "row", "col"),
        P("row", "col"),
        P(None, "row", "col"),
        P(None, "row", "col"),
    )
    out_specs = P("row", "col")
    return jax.shard_map(local, mesh=mesh, in_specs=in_specs, out_specs=out_specs, check_vma=False)
```

```python
import functools

import jax
import jax.numpy as jnp
from jax import lax
from jax.experimental import pallas as pl
from jax.experimental.pallas import tpu as pltpu
from jax.sharding import PartitionSpec as P

STEPS = 4
PIECES = 2
DISCOUNT = 0.97
MESH = pl.DeviceIdType.MESH


def kernel(
    rows, cols, t_ref, v_ref, e_ref, c_ref, out_ref, relay,
    slots, v_buf, work, arrived, e_buf, c_buf,
    in_sem, own_sem, slot_sem, first_sem, up_sem, down_sem, sum_send, sum_recv,
    relay_sem, pass_sem, give_sem,
):
    b = lax.axis_index("row")
    z = lax.axis_index("col")
    ratio = rows // cols
    q = b // ratio
    actions = t_ref.shape[0]
    width = v_ref.shape[0]
    half = width // PIECES
    sums = (STEPS - 1) * actions
    total = STEPS * actions

    loads = [
        pltpu.make_async_copy(v_ref, v_buf, in_sem.at[0]),
        pltpu.make_async_copy(e_ref, e_buf, in_sem.at[1]),
        pltpu.make_async_copy(c_ref, c_buf, in_sem.at[2]),
    ]
    for load in loads:
        load.start()

    barrier = pltpu.get_barrier_semaphore()
    for by in range(1, rows):
        pl.semaphore_signal(barrier, inc=1, device_id=((b + by) % rows, z), device_id_type=MESH)

    @pl.when(z > 0)
    def _():
        pl.semaphore_signal(barrier, inc=1, device_id=(b, z - 1), device_id_type=MESH)

    @pl.when(z < cols - 1)
    def _():
        pl.semaphore_signal(barrier, inc=1, device_id=(b, z + 1), device_id_type=MESH)

    beside = jnp.where(z > 0, 1, 0) + jnp.where(z < cols - 1, 1, 0)
    pl.semaphore_wait(barrier, rows - 1 + beside)

    def held(j, a, h):
        offset = pl.multiple_of(j * width + h * half, 128)
        return t_ref.at[a, :, pl.ds(offset, half)]

    def first_copy(j, d, a, h):
        i = (d - 1) * actions + a
        return pltpu.make_async_remote_copy(
            src_ref=held(j, a, h), dst_ref=slots.at[i, h],
            send_sem=first_sem.at[j, a, h], recv_sem=slot_sem.at[i, h],
            device_id=(z * ratio + j, z), device_id_type=MESH,
        )

    def own_copy(j, a, h):
        i = (STEPS - 1) * actions + a
        return pltpu.make_async_copy(held(j, a, h), slots.at[i, h], own_sem.at[a, h])

    def for_blocks(away, own):
        for j in range(ratio):
            d = (z * ratio + j - b + rows) % rows

            @pl.when((d > 0) & (d < STEPS))
            def _():
                @pl.loop(0, actions)
                def _(a):
                    for h in range(PIECES):
                        away(j, d, a, h)

            if own is not None:
                @pl.when(d == 0)
                def _():
                    @pl.loop(0, actions)
                    def _(a):
                        for h in range(PIECES):
                            own(j, a, h)

    for_blocks(
        lambda j, d, a, h: first_copy(j, d, a, h).start(),
        lambda j, a, h: own_copy(j, a, h).start(),
    )

    def along(i, h, by, sem):
        return pltpu.make_async_remote_copy(
            src_ref=slots.at[i, h], dst_ref=slots.at[i, h],
            send_sem=sem.at[i, h], recv_sem=slot_sem.at[i, h],
            device_id=(b, z + by), device_id_type=MESH,
        )

    goes_up = (z >= q) & (z < cols - 1)
    goes_down = (z <= q) & (z > 0)

    def sum_copy(i):
        d = i // actions + 1
        return pltpu.make_async_remote_copy(
            src_ref=work.at[i], dst_ref=arrived.at[i],
            send_sem=sum_send.at[i], recv_sem=sum_recv.at[i],
            device_id=((b - d + rows) % rows, z), device_id_type=MESH,
        )

    core = b % ratio
    source = z == q
    feeds_up = source & (z < cols - 1)
    feeds_down = source & (z > 0)

    def to_helper(i, h, up):
        u = q if up else cols - 1 - q
        row = ((cols - 1) * ratio if up else 0) + core
        return pltpu.make_async_remote_copy(
            src_ref=slots.at[i, h], dst_ref=relay.at[u, i // actions, h],
            send_sem=(up_sem if up else down_sem).at[i, h],
            recv_sem=relay_sem.at[u, i // actions, h],
            device_id=(row, z), device_id_type=MESH,
        )

    def passed(u, p, h, up):
        return pltpu.make_async_remote_copy(
            src_ref=relay.at[u, p, h], dst_ref=relay.at[u, p, h],
            send_sem=pass_sem.at[u, p, h], recv_sem=relay_sem.at[u, p, h],
            device_id=(b, z + (1 if up else -1)), device_id_type=MESH,
        )

    def given(u, p, h, up):
        row = (u if up else cols - 1 - u) * ratio + core
        return pltpu.make_async_remote_copy(
            src_ref=relay.at[u, p, h], dst_ref=slots.at[p * actions, h],
            send_sem=give_sem.at[u, p, h], recv_sem=slot_sem.at[p * actions, h],
            device_id=(row, z), device_id_type=MESH,
        )

    def for_relay(r, u, finish):
        p = r // actions
        for up in (True, False):
            y = z if up else cols - 1 - z
            helps = (q == (cols - 1 if up else 0)) & (u <= y) & (u < cols - 1)

            @pl.when(helps)
            def _():
                for h in range(PIECES):
                    if not finish:
                        passed(u, p, h, up).wait_recv()

                    @pl.when(y < cols - 1)
                    def _():
                        copy = passed(u, p, h, up)
                        copy.wait_send() if finish else copy.start()

                    @pl.when(y > u)
                    def _():
                        copy = given(u, p, h, up)
                        copy.wait_send() if finish else copy.start()

    per_step = -(-(cols - 1) // actions)

    def relay_step(r, finish):
        @pl.when((r >= 0) & (r < total))
        def _():
            for extra in range(per_step):
                for_relay(r, r % actions + extra * actions, finish)

    def slot_of(s):
        first = jnp.where(source, 0, 1)
        return s // actions * actions + (s % actions + first) % actions

    def own_step(s):
        i = slot_of(s)
        direct = i % actions > 0
        for h in range(PIECES):
            local = (i >= sums) & source

            @pl.when(local)
            def _():
                own_copy(core, i % actions, h).wait()

            @pl.when(jnp.logical_not(local))
            def _():
                along(i, h, 0, up_sem).wait_recv()

            @pl.when(goes_up & direct)
            def _():
                along(i, h, 1, up_sem).start()

            @pl.when(goes_down & direct)
            def _():
                along(i, h, -1, down_sem).start()

            @pl.when(feeds_up & jnp.logical_not(direct))
            def _():
                to_helper(i, h, True).start()

            @pl.when(feeds_down & jnp.logical_not(direct))
            def _():
                to_helper(i, h, False).start()

            tile = 512

            @pl.loop(0, work.shape[2] // tile)
            def _(n):
                at = pl.ds(pl.multiple_of(n * tile, tile), tile)
                product = jnp.dot(
                    slots[i, h], v_buf[h * half:(h + 1) * half, at],
                    preferred_element_type=jnp.float32,
                )
                if h == 0:
                    work[i, :, at] = product
                else:
                    work[i, :, at] += product

        @pl.when((s >= 1) & (s <= sums))
        def _():
            sum_copy(slot_of(s - 1)).start()

    loads[0].wait()
    lag = 2 * jnp.where(q == 0, cols - 1 - z, z)

    @pl.loop(0, total + 2 * cols)
    def _(t):
        relay_step(t - lag, False)

        @pl.when((t >= cols) & (t < cols + total))
        def _():
            own_step(t - cols)

    loads[1].wait()
    loads[2].wait()

    @pl.loop(0, sums)
    def _(i):
        sum_copy(i).wait_recv()

    @pl.loop(0, out_ref.shape[0] // 16)
    def _(k):
        at = pl.ds(pl.multiple_of(k * 16, 16), 16)
        best = None
        for a in range(actions):
            backup = e_buf[a, at, :].astype(jnp.float32) + work[sums + a, at, :]
            for d in range(STEPS - 1):
                backup = backup + arrived[d * actions + a, at, :]
            cost = c_buf[a, at, :].astype(jnp.float32) + DISCOUNT * backup
            best = cost if best is None else jnp.minimum(best, cost)
        out_ref[at, :] = best

    @pl.loop(0, sums)
    def _(i):
        sum_copy(i).wait_send()

    for_blocks(lambda j, d, a, h: first_copy(j, d, a, h).wait_send(), None)

    @pl.loop(0, total)
    def _(i):
        direct = i % actions > 0
        for h in range(PIECES):
            @pl.when((goes_up & direct) | (feeds_up & jnp.logical_not(direct)))
            def _():
                along(i, h, 1, up_sem).wait_send()

            @pl.when((goes_down & direct) | (feeds_down & jnp.logical_not(direct)))
            def _():
                along(i, h, -1, down_sem).wait_send()

        relay_step(i, True)


def local(transitions, values, earlier_sum, section_costs):
    rows = lax.axis_size("row")
    cols = lax.axis_size("col")
    actions, height, _ = transitions.shape
    width, scenarios = values.shape
    total = STEPS * actions
    sums = (STEPS - 1) * actions
    ratio = rows // cols
    anywhere = pl.BlockSpec(memory_space=pl.ANY)
    dma = pltpu.SemaphoreType.DMA
    return pl.pallas_call(
        functools.partial(kernel, rows, cols),
        out_shape=(
            jax.ShapeDtypeStruct((height, scenarios), jnp.float32),
            jax.ShapeDtypeStruct(
                (cols - 1, STEPS, PIECES, height, width // PIECES), jnp.bfloat16
            ),
        ),
        in_specs=[anywhere] * 4,
        out_specs=(pl.BlockSpec(memory_space=pltpu.VMEM), anywhere),
        scratch_shapes=[
            pltpu.VMEM((total, PIECES, height, width // PIECES), jnp.bfloat16),
            pltpu.VMEM((width, scenarios), jnp.bfloat16),
            pltpu.VMEM((total, height, scenarios), jnp.float32),
            pltpu.VMEM((sums, height, scenarios), jnp.float32),
            pltpu.VMEM((actions, height, scenarios), jnp.bfloat16),
            pltpu.VMEM((actions, height, scenarios), jnp.bfloat16),
            dma((3,)),
            dma((actions, PIECES)),
            dma((total, PIECES)),
            dma((ratio, actions, PIECES)),
            dma((total, PIECES)),
            dma((total, PIECES)),
            dma((sums,)),
            dma((sums,)),
            dma((cols - 1, STEPS, PIECES)),
            dma((cols - 1, STEPS, PIECES)),
            dma((cols - 1, STEPS, PIECES)),
        ],
        compiler_params=pltpu.CompilerParams(
            collective_id=0, has_side_effects=True, vmem_limit_bytes=66_000_000
        ),
    )(transitions, values, earlier_sum, section_costs)[0]


def solution(mesh):
    in_specs = (
        P(None, "row", "col"),
        P("row", "col"),
        P(None, "row", "col"),
        P(None, "row", "col"),
    )
    out_specs = P("row", "col")
    return jax.shard_map(local, mesh=mesh, in_specs=in_specs, out_specs=out_specs, check_vma=False)
```

```python
import functools

import jax
import jax.numpy as jnp
from jax import lax
from jax.experimental import pallas as pl
from jax.experimental.pallas import tpu as pltpu
from jax.sharding import PartitionSpec as P

STEPS = 4
PIECES = 4
DISCOUNT = 0.97
MESH = pl.DeviceIdType.MESH


def kernel(
    rows, cols, t_ref, v_ref, e_ref, c_ref, out_ref,
    slots, v_buf, work, arrived, e_buf, c_buf,
    in_sem, own_sem, slot_sem, first_sem, up_sem, down_sem, sum_send, sum_recv,
):
    b = lax.axis_index("row")
    z = lax.axis_index("col")
    ratio = rows // cols
    q = b // ratio
    actions = t_ref.shape[0]
    width = v_ref.shape[0]
    half = width // PIECES
    sums = (STEPS - 1) * actions
    total = STEPS * actions

    loads = [
        pltpu.make_async_copy(v_ref, v_buf, in_sem.at[0]),
        pltpu.make_async_copy(e_ref, e_buf, in_sem.at[1]),
        pltpu.make_async_copy(c_ref, c_buf, in_sem.at[2]),
    ]
    for load in loads:
        load.start()

    barrier = pltpu.get_barrier_semaphore()
    for d in range(1, STEPS):
        for by in (d, rows - d):
            pl.semaphore_signal(barrier, inc=1, device_id=((b + by) % rows, z), device_id_type=MESH)

    @pl.when(z > 0)
    def _():
        pl.semaphore_signal(barrier, inc=1, device_id=(b, z - 1), device_id_type=MESH)

    @pl.when(z < cols - 1)
    def _():
        pl.semaphore_signal(barrier, inc=1, device_id=(b, z + 1), device_id_type=MESH)

    beside = jnp.where(z > 0, 1, 0) + jnp.where(z < cols - 1, 1, 0)
    pl.semaphore_wait(barrier, 2 * (STEPS - 1) + beside)

    def held(j, a, h):
        offset = pl.multiple_of(j * width + h * half, 128)
        return t_ref.at[a, :, pl.ds(offset, half)]

    def first_copy(j, d, a, h):
        i = (d - 1) * actions + a
        return pltpu.make_async_remote_copy(
            src_ref=held(j, a, h), dst_ref=slots.at[i, h],
            send_sem=first_sem.at[j, a, h], recv_sem=slot_sem.at[i, h],
            device_id=(z * ratio + j, z), device_id_type=MESH,
        )

    def own_copy(j, a, h):
        i = (STEPS - 1) * actions + a
        return pltpu.make_async_copy(held(j, a, h), slots.at[i, h], own_sem.at[a, h])

    def for_blocks(away, own):
        for j in range(ratio):
            d = (z * ratio + j - b + rows) % rows

            @pl.when((d > 0) & (d < STEPS))
            def _():
                @pl.loop(0, actions)
                def _(a):
                    for h in range(PIECES):
                        away(j, d, a, h)

            if own is not None:
                @pl.when(d == 0)
                def _():
                    @pl.loop(0, actions)
                    def _(a):
                        for h in range(PIECES):
                            own(j, a, h)

    for_blocks(
        lambda j, d, a, h: first_copy(j, d, a, h).start(),
        lambda j, a, h: own_copy(j, a, h).start(),
    )

    def along(i, h, by, sem):
        return pltpu.make_async_remote_copy(
            src_ref=slots.at[i, h], dst_ref=slots.at[i, h],
            send_sem=sem.at[i, h], recv_sem=slot_sem.at[i, h],
            device_id=(b, z + by), device_id_type=MESH,
        )

    goes_up = (z >= q) & (z < cols - 1)
    goes_down = (z <= q) & (z > 0)

    def sum_copy(i):
        d = i // actions + 1
        return pltpu.make_async_remote_copy(
            src_ref=work.at[i], dst_ref=arrived.at[i],
            send_sem=sum_send.at[i], recv_sem=sum_recv.at[i],
            device_id=((b - d + rows) % rows, z), device_id_type=MESH,
        )

    def finish(a):
        for d in range(STEPS - 1):
            sum_copy(d * actions + a).wait_recv()

        @pl.loop(0, out_ref.shape[0] // 16)
        def _(k):
            at = pl.ds(pl.multiple_of(k * 16, 16), 16)
            backup = e_buf[a, at, :].astype(jnp.float32) + work[sums + a, at, :]
            for d in range(STEPS - 1):
                backup = backup + arrived[d * actions + a, at, :]
            cost = c_buf[a, at, :].astype(jnp.float32) + DISCOUNT * backup

            @pl.when(a == 0)
            def _():
                out_ref[at, :] = cost

            @pl.when(a > 0)
            def _():
                out_ref[at, :] = jnp.minimum(out_ref[at, :], cost)

    @pl.loop(0, total)
    def _(i):
        for h in range(PIECES):
            local = (i >= sums) & (z == q)

            @pl.when(local)
            def _():
                own_copy(b % ratio, i % actions, h).wait()

            @pl.when(jnp.logical_not(local))
            def _():
                along(i, h, 0, up_sem).wait_recv()

            @pl.when(goes_up)
            def _():
                along(i, h, 1, up_sem).start()

            @pl.when(goes_down)
            def _():
                along(i, h, -1, down_sem).start()

            if h == 0:
                @pl.when(i == 0)
                def _():
                    for load in loads:
                        load.wait()

            tile = 512

            @pl.loop(0, work.shape[2] // tile)
            def _(n):
                at = pl.ds(pl.multiple_of(n * tile, tile), tile)
                product = jnp.dot(
                    slots[i, h], v_buf[h * half:(h + 1) * half, at],
                    preferred_element_type=jnp.float32,
                )
                if h == 0:
                    work[i, :, at] = product
                else:
                    work[i, :, at] += product

        @pl.when((i >= 1) & (i <= sums))
        def _():
            sum_copy(i - 1).start()

        @pl.when(i > sums)
        def _():
            finish(i - 1 - sums)

    finish(actions - 1)

    @pl.loop(0, sums)
    def _(i):
        sum_copy(i).wait_send()

    for_blocks(lambda j, d, a, h: first_copy(j, d, a, h).wait_send(), None)

    @pl.when(goes_up)
    def _():
        @pl.loop(0, total)
        def _(i):
            for h in range(PIECES):
                along(i, h, 1, up_sem).wait_send()

    @pl.when(goes_down)
    def _():
        @pl.loop(0, total)
        def _(i):
            for h in range(PIECES):
                along(i, h, -1, down_sem).wait_send()


def local(transitions, values, earlier_sum, section_costs):
    rows = lax.axis_size("row")
    cols = lax.axis_size("col")
    actions, height, _ = transitions.shape
    width, scenarios = values.shape
    total = STEPS * actions
    sums = (STEPS - 1) * actions
    ratio = rows // cols
    anywhere = pl.BlockSpec(memory_space=pl.ANY)
    dma = pltpu.SemaphoreType.DMA
    return pl.pallas_call(
        functools.partial(kernel, rows, cols),
        out_shape=jax.ShapeDtypeStruct((height, scenarios), jnp.float32),
        in_specs=[anywhere] * 4,
        out_specs=pl.BlockSpec(memory_space=pltpu.VMEM),
        scratch_shapes=[
            pltpu.VMEM((total, PIECES, height, width // PIECES), jnp.bfloat16),
            pltpu.VMEM((width, scenarios), jnp.bfloat16),
            pltpu.VMEM((total, height, scenarios), jnp.float32),
            pltpu.VMEM((sums, height, scenarios), jnp.float32),
            pltpu.VMEM((actions, height, scenarios), jnp.bfloat16),
            pltpu.VMEM((actions, height, scenarios), jnp.bfloat16),
            dma((3,)),
            dma((actions, PIECES)),
            dma((total, PIECES)),
            dma((ratio, actions, PIECES)),
            dma((total, PIECES)),
            dma((total, PIECES)),
            dma((sums,)),
            dma((sums,)),
        ],
        compiler_params=pltpu.CompilerParams(
            collective_id=0, has_side_effects=True, vmem_limit_bytes=66_000_000
        ),
    )(transitions, values, earlier_sum, section_costs)


def solution(mesh):
    in_specs = (
        P(None, "row", "col"),
        P("row", "col"),
        P(None, "row", "col"),
        P(None, "row", "col"),
    )
    out_specs = P("row", "col")
    return jax.shard_map(local, mesh=mesh, in_specs=in_specs, out_specs=out_specs, check_vma=False)
```

```python
import functools

import jax
import jax.numpy as jnp
from jax import lax
from jax.experimental import pallas as pl
from jax.experimental.pallas import tpu as pltpu
from jax.sharding import PartitionSpec as P

STEPS = 4
PIECES = 8
DISCOUNT = 0.97
MESH = pl.DeviceIdType.MESH


def kernel(
    rows, cols, t_ref, v_ref, e_ref, c_ref, out_ref,
    slots, v_buf, work, arrived, e_buf, c_buf,
    in_sem, own_sem, slot_sem, first_sem, up_sem, down_sem, sum_send, sum_recv,
):
    b = lax.axis_index("row")
    z = lax.axis_index("col")
    ratio = rows // cols
    q = b // ratio
    actions = t_ref.shape[0]
    width = v_ref.shape[0]
    half = width // PIECES
    sums = (STEPS - 1) * actions
    total = STEPS * actions

    loads = [
        pltpu.make_async_copy(v_ref, v_buf, in_sem.at[0]),
        pltpu.make_async_copy(e_ref, e_buf, in_sem.at[1]),
        pltpu.make_async_copy(c_ref, c_buf, in_sem.at[2]),
    ]
    for load in loads:
        load.start()

    barrier = pltpu.get_barrier_semaphore()
    for d in range(1, STEPS):
        for by in (d, rows - d):
            pl.semaphore_signal(barrier, inc=1, device_id=((b + by) % rows, z), device_id_type=MESH)

    @pl.when(z > 0)
    def _():
        pl.semaphore_signal(barrier, inc=1, device_id=(b, z - 1), device_id_type=MESH)

    @pl.when(z < cols - 1)
    def _():
        pl.semaphore_signal(barrier, inc=1, device_id=(b, z + 1), device_id_type=MESH)

    beside = jnp.where(z > 0, 1, 0) + jnp.where(z < cols - 1, 1, 0)
    pl.semaphore_wait(barrier, 2 * (STEPS - 1) + beside)

    def held(j, a, h):
        offset = pl.multiple_of(j * width + h * half, 128)
        return t_ref.at[a, :, pl.ds(offset, half)]

    def first_copy(j, d, a, h):
        i = (d - 1) * actions + a
        return pltpu.make_async_remote_copy(
            src_ref=held(j, a, h), dst_ref=slots.at[i, h],
            send_sem=first_sem.at[j, a, h], recv_sem=slot_sem.at[i, h],
            device_id=(z * ratio + j, z), device_id_type=MESH,
        )

    def own_copy(j, a, h):
        i = (STEPS - 1) * actions + a
        return pltpu.make_async_copy(held(j, a, h), slots.at[i, h], own_sem.at[a, h])

    def for_blocks(away, own):
        for j in range(ratio):
            d = (z * ratio + j - b + rows) % rows

            @pl.when((d > 0) & (d < STEPS))
            def _():
                @pl.loop(0, actions)
                def _(a):
                    for h in range(PIECES):
                        away(j, d, a, h)

            if own is not None:
                @pl.when(d == 0)
                def _():
                    @pl.loop(0, actions)
                    def _(a):
                        for h in range(PIECES):
                            own(j, a, h)

    for_blocks(
        lambda j, d, a, h: first_copy(j, d, a, h).start(),
        lambda j, a, h: own_copy(j, a, h).start(),
    )

    def along(i, h, by, sem):
        return pltpu.make_async_remote_copy(
            src_ref=slots.at[i, h], dst_ref=slots.at[i, h],
            send_sem=sem.at[i, h], recv_sem=slot_sem.at[i, h],
            device_id=(b, z + by), device_id_type=MESH,
        )

    goes_up = (z >= q) & (z < cols - 1)
    goes_down = (z <= q) & (z > 0)

    def sum_copy(i):
        d = i // actions + 1
        return pltpu.make_async_remote_copy(
            src_ref=work.at[i], dst_ref=arrived.at[i],
            send_sem=sum_send.at[i], recv_sem=sum_recv.at[i],
            device_id=((b - d + rows) % rows, z), device_id_type=MESH,
        )

    def finish(a):
        for d in range(STEPS - 1):
            sum_copy(d * actions + a).wait_recv()

        @pl.loop(0, out_ref.shape[0] // 16)
        def _(k):
            at = pl.ds(pl.multiple_of(k * 16, 16), 16)
            backup = e_buf[a, at, :].astype(jnp.float32) + work[sums + a, at, :]
            for d in range(STEPS - 1):
                backup = backup + arrived[d * actions + a, at, :]
            cost = c_buf[a, at, :].astype(jnp.float32) + DISCOUNT * backup

            @pl.when(a == 0)
            def _():
                out_ref[at, :] = cost

            @pl.when(a > 0)
            def _():
                out_ref[at, :] = jnp.minimum(out_ref[at, :], cost)

    @pl.loop(0, total)
    def _(i):
        for h in range(PIECES):
            local = (i >= sums) & (z == q)

            @pl.when(local)
            def _():
                own_copy(b % ratio, i % actions, h).wait()

            @pl.when(jnp.logical_not(local))
            def _():
                along(i, h, 0, up_sem).wait_recv()

            @pl.when(goes_up)
            def _():
                along(i, h, 1, up_sem).start()

            @pl.when(goes_down)
            def _():
                along(i, h, -1, down_sem).start()

            if h == 0:
                @pl.when(i == 0)
                def _():
                    for load in loads:
                        load.wait()

            tile = 512

            @pl.loop(0, work.shape[2] // tile)
            def _(n):
                at = pl.ds(pl.multiple_of(n * tile, tile), tile)
                product = jnp.dot(
                    slots[i, h], v_buf[h * half:(h + 1) * half, at],
                    preferred_element_type=jnp.float32,
                )
                if h == 0:
                    work[i, :, at] = product
                else:
                    work[i, :, at] += product

        @pl.when((i >= 1) & (i <= sums))
        def _():
            sum_copy(i - 1).start()

        @pl.when(i > sums)
        def _():
            finish(i - 1 - sums)

    finish(actions - 1)

    @pl.loop(0, sums)
    def _(i):
        sum_copy(i).wait_send()

    for_blocks(lambda j, d, a, h: first_copy(j, d, a, h).wait_send(), None)

    @pl.when(goes_up)
    def _():
        @pl.loop(0, total)
        def _(i):
            for h in range(PIECES):
                along(i, h, 1, up_sem).wait_send()

    @pl.when(goes_down)
    def _():
        @pl.loop(0, total)
        def _(i):
            for h in range(PIECES):
                along(i, h, -1, down_sem).wait_send()


def local(transitions, values, earlier_sum, section_costs):
    rows = lax.axis_size("row")
    cols = lax.axis_size("col")
    actions, height, _ = transitions.shape
    width, scenarios = values.shape
    total = STEPS * actions
    sums = (STEPS - 1) * actions
    ratio = rows // cols
    anywhere = pl.BlockSpec(memory_space=pl.ANY)
    dma = pltpu.SemaphoreType.DMA
    return pl.pallas_call(
        functools.partial(kernel, rows, cols),
        out_shape=jax.ShapeDtypeStruct((height, scenarios), jnp.float32),
        in_specs=[anywhere] * 4,
        out_specs=pl.BlockSpec(memory_space=pltpu.VMEM),
        scratch_shapes=[
            pltpu.VMEM((total, PIECES, height, width // PIECES), jnp.bfloat16),
            pltpu.VMEM((width, scenarios), jnp.bfloat16),
            pltpu.VMEM((total, height, scenarios), jnp.float32),
            pltpu.VMEM((sums, height, scenarios), jnp.float32),
            pltpu.VMEM((actions, height, scenarios), jnp.bfloat16),
            pltpu.VMEM((actions, height, scenarios), jnp.bfloat16),
            dma((3,)),
            dma((actions, PIECES)),
            dma((total, PIECES)),
            dma((ratio, actions, PIECES)),
            dma((total, PIECES)),
            dma((total, PIECES)),
            dma((sums,)),
            dma((sums,)),
        ],
        compiler_params=pltpu.CompilerParams(
            collective_id=0, has_side_effects=True, vmem_limit_bytes=66_000_000
        ),
    )(transitions, values, earlier_sum, section_costs)


def solution(mesh):
    in_specs = (
        P(None, "row", "col"),
        P("row", "col"),
        P(None, "row", "col"),
        P(None, "row", "col"),
    )
    out_specs = P("row", "col")
    return jax.shard_map(local, mesh=mesh, in_specs=in_specs, out_specs=out_specs, check_vma=False)
```
